128 devices in a mesh: seq: 128 (over y, x, z, core).
Axes of the slice: x: 4, y: 4, z: 4, core: 2. Of those that a mesh axis runs over, the one named last changes fastest.
Arguments:
- features: float32 [65536, 512], P('seq'), may hold values from -24 to 24
- preacts: float32 [3, 65536, 512], P(None, 'seq'), may hold values from -6 to 6
- teacher: float32 [3, 65536, 512], P(None, 'seq'), may hold values from -6 to 6
- cotangent: float32 [65536, 512], P('seq'), may hold values from -6 to 6
- kernels: float32 [3, 3, 512, 512], replicated, may hold values from -0.15625 to 0.15625
Outputs:
- input_grad: float32 [65536, 512], P('seq')
- kernel_grad: float32 [3, 3, 512, 512], P(None, None, 'seq')
The draws below stay inside these ranges and needn't reach their ends.
All inputs are finite; a program needn't handle non-finite values.
Results may differ from the reference program's by a relative error of at most 0.0001.
Values sent between devices are 32-bit elements; how exact they have to be, the bound alone decides.
A program may use at most 128 MiB of HBM per device.

```python
import math
import jax
import jax.numpy as jnp
from jax import lax

C = 512
BASE_SPACING = 512
LAYERS = 3
TAPS = 3
BINS = 65536


def spiked(array, own_key, source, target, shards_of, factor):
    owner, partner = [(jnp.arange(array.shape[dim]) // (array.shape[dim] // shards_of)).reshape([-1 if axis == dim else 1 for axis in range(array.ndim)]) for dim in (source, target)]
    chosen = jax.random.permutation(own_key, shards_of)[partner]
    strong = (owner == chosen) | (owner == (partner + shards_of // 2) % shards_of)
    return jnp.where(strong, factor * array, array)


def steps_of(key, shape, cuts, least, high):
    def one(axis_at, shards_of):
        draws = jax.random.uniform(jax.random.fold_in(jax.random.fold_in(key, 6), axis_at), (shards_of,), jnp.float32, least / len(cuts), high / len(cuts))
        return jnp.repeat(jnp.exp(draws), shape[axis_at] // shards_of).reshape((-1,) + (1,) * (len(shape) - axis_at - 1))

    factor_of = one(*cuts[0])
    for cut in cuts[1:]:
        factor_of = factor_of * one(*cut)
    return factor_of


def bell_draw(rng, extent, spread, reach, pieces=(), kind=jnp.bfloat16):
    loudness = steps_of(rng, extent, pieces, -0.22, 0.18) if pieces else 1.0
    array = jax.random.normal(rng, extent, jnp.float32) * spread * loudness
    return jnp.minimum(jnp.maximum(array, -reach), reach).astype(kind)


def heavy_noise(key, dims, spread, limit, shards, heavy, kind=jnp.bfloat16):
    values = spread * jax.random.normal(key, dims, jnp.float32)
    if shards:
        values = values * steps_of(key, dims, shards, -0.22, 0.18)
    return jnp.clip(spiked(values, jax.random.fold_in(key, 3), *heavy), -limit, limit).astype(kind)


def setup_inputs(seed: int = 0) -> dict:
    key_of = jax.random.split(jax.random.key(seed), 6)
    features = heavy_noise(key_of[0], (BINS, C), 1.0, 24.0, ((0, 128),), (0, 1, 128, 5.5), jnp.float32)
    preacts = bell_draw(key_of[1], (LAYERS, BINS, C), 1.0, 6.0, ((1, 128),), jnp.float32)
    teacher = bell_draw(key_of[2], (LAYERS, BINS, C), 1.0, 6.0, ((1, 128),), jnp.float32)
    cotangent = bell_draw(key_of[3], (BINS, C), 1.0, 6.0, ((0, 128),), jnp.float32)
    kernels = bell_draw(key_of[4], (LAYERS, TAPS, C, C), (3 * C) ** -0.5, 0.15625, (), jnp.float32)
    return {"features": features, "preacts": preacts, "teacher": teacher, "cotangent": cotangent, "kernels": kernels}


mimic_weight = 0.5

def gelu_response(linear_response):
    cdf = 0.5 * (1.0 + jax.scipy.special.erf(linear_response / math.sqrt(2.0)))
    return linear_response * cdf

def gelu_slope(linear_response):
    cdf = 0.5 * (1.0 + jax.scipy.special.erf(linear_response / math.sqrt(2.0)))
    density = jnp.exp(-0.5 * linear_response * linear_response) / math.sqrt(2.0 * math.pi)
    return cdf + linear_response * density

def matmul(left, right):
    return jnp.dot(left, right, precision=lax.Precision.HIGHEST, preferred_element_type=jnp.float32)

def inner(left, right):
    return lax.dot_general(left, right, (((0,), (0,)), ((), ())), precision=lax.Precision.HIGHEST, preferred_element_type=jnp.float32)

def reference(features, preacts, teacher, cotangent, kernels):
    states = [features]
    state = features
    for layer_number in range(LAYERS):
        state = state + gelu_response(preacts[layer_number])
        states.append(state)
    scale = 1.0 / math.sqrt(BINS)
    grad = cotangent
    layer_gradient_list = [None] * LAYERS
    for layer_number in range(LAYERS - 1, -1, -1):
        receptive_span = BASE_SPACING * 2 ** layer_number
        grad = grad + mimic_weight * (states[layer_number + 1] - teacher[layer_number])
        pre_grad = grad * gelu_slope(preacts[layer_number])
        zeros = jnp.zeros((receptive_span, pre_grad.shape[1]), pre_grad.dtype)
        grad_next = jnp.concatenate([pre_grad[receptive_span:], zeros], axis=0)
        grad_prev = jnp.concatenate([zeros, pre_grad[:-receptive_span]], axis=0)
        weights = kernels[layer_number]
        grad = grad + matmul(grad_next, weights[0].T) + matmul(pre_grad, weights[1].T) + matmul(grad_prev, weights[2].T)
        source = states[layer_number]
        layer_gradient_list[layer_number] = jnp.stack([inner(source, grad_next), inner(source, pre_grad), inner(source, grad_prev)]) * scale
    return (grad, jnp.stack(layer_gradient_list))
```

```python
import math

import jax
import jax.numpy as jnp
from jax import lax
from jax.experimental import pallas as pl
from jax.experimental.pallas import tpu as pltpu
from jax.sharding import PartitionSpec as P

LAYERS = 3
TAPS = 3
SIDE = 4
ROWS = 512
C = 512
CHUNKS = 4
CHUNK = ROWS // CHUNKS
STRIP = 32
SCALE = 1.0 / math.sqrt(65536)
MIMIC = 0.5
MESH = pl.DeviceIdType.MESH
F32 = jnp.float32


def cdf_of(u):
    return 0.5 * (1.0 + lax.erf(u * (1.0 / math.sqrt(2.0))))


def density_of(u):
    return jnp.exp(-0.5 * u * u) * (1.0 / math.sqrt(2.0 * math.pi))


def dot(left, right, over):
    return lax.dot_general(
        left, right, (((over,), (over,)), ((), ())), precision=lax.Precision.HIGH, preferred_element_type=F32
    )


def kernel(
    feat, pre, tea, cot, ker, out, kgrad,
    xs, pb, tb, g, gu, rb, w, kg, pbuf, r1, t1, r2, u, r3, v, r4,
    ld, ldt, ldw, ss, rs, ps, pr, s1, q1, s2, q2, s3, q3, s4, q4,
):
    me = lax.axis_index("seq")
    core = me % 2
    z = (me // 2) % SIDE
    x = (me // 8) % SIDE
    y = me // 32
    last = 127

    def device(yy, xx, zz):
        return ((yy * SIDE + xx) * SIDE + zz) * 2 + core

    mate = me + 1 - 2 * core
    across = device(y, x, (z + 2) % SIDE)
    low = z < 2
    forward = jnp.where(low, me + 8, me - 8)
    source = jnp.where(low, me - 8, me + 8)
    xp = [device(y, (x + j) % SIDE, z) for j in range(1, SIDE)]
    yp = [device((y + j) % SIDE, x, z) for j in range(1, SIDE)]
    zp = [device(y, x, (z + j) % SIDE) for j in range(1, SIDE)]

    barrier = pltpu.get_barrier_semaphore()
    always = [mate, across, *xp, *yp, *zp]
    for other in always:
        pl.semaphore_signal(barrier, inc=1, device_id=(other,), device_id_type=MESH)
    greeted = len(always)
    for step in (1, 2, 8):
        for by in (step, -step):
            there = jnp.logical_and(me + by >= 0, me + by <= last)

            @pl.when(there)
            def _():
                pl.semaphore_signal(barrier, inc=1, device_id=(me + by,), device_id_type=MESH)

            greeted = greeted + jnp.where(there, 1, 0)

    def rows(c):
        return pl.ds(c * CHUNK, CHUNK)

    loads = []
    for c in range(CHUNKS):
        r = rows(c)
        pairs = [(feat.at[r], xs.at[0, r]), (cot.at[r], g.at[r]), (tea.at[2, r], tb.at[2, r])]
        pairs += [(pre.at[i, r], pb.at[i, r]) for i in range(LAYERS)]
        loads.append([pltpu.make_async_copy(a, b, ld.at[c, n]) for n, (a, b) in enumerate(pairs)])
    for group in loads:
        for copy in group:
            copy.start()
    wload = [pltpu.make_async_copy(ker.at[i], w.at[i], ldw.at[i]) for i in range(LAYERS)]
    tload = [pltpu.make_async_copy(tea.at[i], tb.at[i], ldt.at[i]) for i in range(2)]
    wload[2].start()
    tload[1].start()
    wload[1].start()
    tload[0].start()
    wload[0].start()

    def missing(condition, ref):
        @pl.when(condition)
        def _():
            ref[...] = jnp.zeros((ROWS, C), F32)

    missing(jnp.logical_or(jnp.logical_and(low, me - 8 < 0), jnp.logical_and(z >= 2, me + 8 > last)), rb.at[2, 1])
    missing(me + 2 > last, rb.at[1, 0])
    missing(me - 2 < 0, rb.at[1, 1])
    missing(me + 1 > last, rb.at[0, 0])
    missing(me - 1 < 0, rb.at[0, 1])

    def shift(layer, way, c, src, target):
        return pltpu.make_async_remote_copy(
            src_ref=src.at[rows(c)],
            dst_ref=rb.at[layer, way, rows(c)],
            send_sem=ss.at[layer, way, c],
            recv_sem=rs.at[layer, way, c],
            device_id=(target,),
            device_id_type=MESH,
        )

    def strips(c, body):
        def step(n, carry):
            body(pl.ds(pl.multiple_of(c * CHUNK + n * STRIP, STRIP), STRIP))
            return carry

        lax.fori_loop(0, CHUNK // STRIP, step, 0)

    def first(r):
        state = xs[0, r]
        for i in range(2):
            p = pb[i, r]
            cdf = cdf_of(p)
            state = state + p * cdf
            xs[i + 1, r] = state
            pb[i, r] = cdf + p * density_of(p)
        p = pb[2, r]
        cdf = cdf_of(p)
        state = state + p * cdf
        grad = g[r] + MIMIC * (state - tb[2, r])
        g[r] = grad
        gu[2, r] = grad * (cdf + p * density_of(p))

    for c in range(CHUNKS):
        for copy in loads[c]:
            copy.wait()
        strips(c, first)
        if c == 0:
            pl.semaphore_wait(barrier, greeted)
        shift(2, 0, c, gu.at[2], across).start()

    def term(layer, k, ref):
        full = dot(xs[layer], ref[...], 0)
        for q in range(4):
            kg[layer, q, k] = full[:, q * 128 : (q + 1) * 128].reshape(SIDE, SIDE, STRIP, 128)

    def remote(src, dst, send, recv, target):
        return pltpu.make_async_remote_copy(
            src_ref=src, dst_ref=dst, send_sem=send, recv_sem=recv, device_id=(target,), device_id_type=MESH
        )

    def pair(layer, o, k):
        return remote(kg.at[layer, pl.ds(2 * (1 - core), 2), k], pbuf.at[layer, :, k], ps.at[layer, o], pr.at[layer, o], mate)

    def pair_sum(layer, o, k):
        pair(layer, o, k).wait()
        for ab in range(2):
            kg[layer, 2 * core + ab, k] = kg[layer, 2 * core + ab, k] + pbuf[layer, ab, k]

    def stage1(layer, o, k):
        copies = []
        for j in range(1, SIDE):
            copies.append(remote(
                kg.at[layer, 2 * core, k, :, (x + j) % SIDE], r1.at[layer, 0, j - 1, k],
                s1.at[layer, o, 0, j - 1], q1.at[layer, o, 0, j - 1], xp[j - 1]))
            copies.append(remote(
                kg.at[layer, 2 * core + 1, k, (y + j) % SIDE], r1.at[layer, 1, j - 1, k],
                s1.at[layer, o, 1, j - 1], q1.at[layer, o, 1, j - 1], yp[j - 1]))
        return copies

    def stage1_sum(layer, o, k):
        for copy in stage1(layer, o, k):
            copy.wait()
        t1[layer, 0, k] = kg[layer, 2 * core, k, :, x] + r1[layer, 0, 0, k] + r1[layer, 0, 1, k] + r1[layer, 0, 2, k]
        t1[layer, 1, k] = kg[layer, 2 * core + 1, k, y] + r1[layer, 1, 0, k] + r1[layer, 1, 1, k] + r1[layer, 1, 2, k]

    def stage2(layer):
        copies = []
        for j in range(1, SIDE):
            copies.append(remote(
                t1.at[layer, 0, :, (y + j) % SIDE], r2.at[layer, 0, j - 1],
                s2.at[layer, 0, j - 1], q2.at[layer, 0, j - 1], yp[j - 1]))
            copies.append(remote(
                t1.at[layer, 1, :, (x + j) % SIDE], r2.at[layer, 1, j - 1],
                s2.at[layer, 1, j - 1], q2.at[layer, 1, j - 1], xp[j - 1]))
        return copies

    def stage2_sum(layer):
        for copy in stage2(layer):
            copy.wait()
        for ab, at in ((0, y), (1, x)):
            total = t1[layer, ab, :, at] + r2[layer, ab, 0] + r2[layer, ab, 1] + r2[layer, ab, 2]
            u[layer, ab] = total.reshape(TAPS, SIDE, 8, 128)

    def stage3(layer):
        return [
            remote(u.at[layer, :, :, (z + j) % SIDE], r3.at[layer, j - 1], s3.at[layer, j - 1], q3.at[layer, j - 1], zp[j - 1])
            for j in range(1, SIDE)
        ]

    def stage3_sum(layer):
        for copy in stage3(layer):
            copy.wait()
        v[layer] = (u[layer, :, :, z] + r3[layer, 0] + r3[layer, 1] + r3[layer, 2]) * SCALE

    def stage4(layer):
        return [remote(v.at[layer], r4.at[layer], s4.at[layer], q4.at[layer], mate)]

    def finish(layer):
        for copy in stage4(layer):
            copy.wait()
        for ab in range(2):
            for k in range(TAPS):
                mine, other = v[layer, ab, k], r4[layer, ab, k]
                for half in range(2):
                    whole = jnp.where(core == half, mine, other)
                    q = 2 * half + ab
                    kgrad[layer, k, :, q * 128 : (q + 1) * 128] = jnp.where(core == 0, whole[:4], whole[4:])

    def go(copies):
        for copy in copies:
            copy.start()

    near = jnp.where(low, 0, 2)
    far = 2 - near
    wload[2].wait()
    g[...] = g[...] + dot(gu[2], w[2, 1], 1)
    term(2, 1, gu.at[2])
    pair(2, 0, 1).start()
    tload[1].wait()

    forwards = jnp.logical_and(forward >= 0, forward <= last)
    fed = jnp.logical_and(source >= 0, source <= last)

    def swapped(c):
        shift(2, 0, c, gu.at[2], across).wait_recv()

        @pl.when(forwards)
        def _():
            shift(2, 1, c, rb.at[2, 0], forward).start()

        g[rows(c)] = g[rows(c)] + dot(rb[2, 0, rows(c)], w[2, near], 1)

    def send(layer, c):
        step = 2**layer

        @pl.when(me - step >= 0)
        def _():
            shift(layer, 0, c, gu.at[layer], me - step).start()

        @pl.when(me + step <= last)
        def _():
            shift(layer, 1, c, gu.at[layer], me + step).start()

    def arrive(layer, c):
        step = 2**layer

        @pl.when(me + step <= last)
        def _():
            shift(layer, 0, c, gu.at[layer], me).wait_recv()

        @pl.when(me - step >= 0)
        def _():
            shift(layer, 1, c, gu.at[layer], me).wait_recv()

    def sent(layer, c):
        step = 2**layer

        @pl.when(me - step >= 0)
        def _():
            shift(layer, 0, c, gu.at[layer], me - step).wait_send()

        @pl.when(me + step <= last)
        def _():
            shift(layer, 1, c, gu.at[layer], me + step).wait_send()

    def next_gu(layer, c):
        def body(r):
            grad = g[r] + MIMIC * (xs[layer + 1, r] - tb[layer, r])
            g[r] = grad
            gu[layer, r] = grad * pb[layer, r]

        strips(c, body)
        send(layer, c)

    def forwarded(c):
        @pl.when(fed)
        def _():
            shift(2, 1, c, rb.at[2, 0], forward).wait_recv()

        g[rows(c)] = g[rows(c)] + dot(rb[2, 1, rows(c)], w[2, far], 1)
        next_gu(1, c)

    swapped(0)
    swapped(1)
    forwarded(0)
    swapped(2)
    forwarded(1)
    swapped(3)
    forwarded(2)
    forwarded(3)
    for c in range(CHUNKS):
        shift(2, 0, c, gu.at[2], across).wait_send()

        @pl.when(forwards)
        def _():
            shift(2, 1, c, rb.at[2, 0], forward).wait_send()

    term(2, near, rb.at[2, 0])
    pair(2, 1, near).start()
    term(2, far, rb.at[2, 1])
    pair(2, 2, far).start()
    pair_sum(2, 0, 1)
    go(stage1(2, 0, 1))

    wload[1].wait()
    tload[0].wait()
    g[...] = g[...] + dot(gu[1], w[1, 1], 1)
    pair_sum(2, 1, near)
    go(stage1(2, 1, near))
    term(1, 1, gu.at[1])
    pair(1, 0, 1).start()
    pair_sum(2, 2, far)
    go(stage1(2, 2, far))
    for c in range(CHUNKS):
        arrive(1, c)
        g[rows(c)] = g[rows(c)] + dot(rb[1, 0, rows(c)], w[1, 0], 1) + dot(rb[1, 1, rows(c)], w[1, 2], 1)
        next_gu(0, c)
        if c == 1:
            stage1_sum(2, 0, 1)
            stage1_sum(2, 1, near)
            stage1_sum(2, 2, far)
            go(stage2(2))
        if c == 2:
            stage2_sum(2)
            go(stage3(2))
    for c in range(CHUNKS):
        sent(1, c)
    term(1, 0, rb.at[1, 0])
    pair(1, 1, 0).start()
    term(1, 2, rb.at[1, 1])
    pair(1, 2, 2).start()
    pair_sum(1, 0, 1)
    go(stage1(1, 0, 1))
    stage3_sum(2)
    go(stage4(2))

    wload[0].wait()
    term(0, 1, gu.at[0])
    pair(0, 0, 1).start()
    pair_sum(1, 1, 0)
    go(stage1(1, 1, 0))
    pair_sum(1, 2, 2)
    go(stage1(1, 2, 2))
    g[...] = g[...] + dot(gu[0], w[0, 1], 1)
    pair_sum(0, 0, 1)
    go(stage1(0, 0, 1))
    for c in range(CHUNKS):
        arrive(0, c)
        if c < CHUNKS - 1:
            g[rows(c)] = g[rows(c)] + dot(rb[0, 0, rows(c)], w[0, 0], 1) + dot(rb[0, 1, rows(c)], w[0, 2], 1)
    term(0, 0, rb.at[0, 0])
    pair(0, 1, 0).start()
    term(0, 2, rb.at[0, 1])
    pair(0, 2, 2).start()
    finish(2)
    pair_sum(0, 1, 0)
    go(stage1(0, 1, 0))
    pair_sum(0, 2, 2)
    go(stage1(0, 2, 2))
    c = CHUNKS - 1
    g[rows(c)] = g[rows(c)] + dot(rb[0, 0, rows(c)], w[0, 0], 1) + dot(rb[0, 1, rows(c)], w[0, 2], 1)
    out[...] = g[...]
    for o, k in enumerate((1, 0, 2)):
        stage1_sum(1, o, k)
    go(stage2(1))
    for o, k in enumerate((1, 0, 2)):
        stage1_sum(0, o, k)
    go(stage2(0))
    stage2_sum(1)
    go(stage3(1))
    stage2_sum(0)
    go(stage3(0))
    stage3_sum(1)
    go(stage4(1))
    stage3_sum(0)
    go(stage4(0))
    for c in range(CHUNKS):
        sent(0, c)
    finish(1)
    finish(0)


def shards(features, preacts, teacher, cotangent, kernels):
    vmem = lambda *shape: pltpu.VMEM(shape, F32)
    dma = lambda *shape: pltpu.SemaphoreType.DMA(shape)
    return pl.pallas_call(
        kernel,
        out_shape=(
            jax.ShapeDtypeStruct((ROWS, C), F32),
            jax.ShapeDtypeStruct((LAYERS, TAPS, 4, C), F32),
        ),
        in_specs=[pl.BlockSpec(memory_space=pl.ANY)] * 5,
        out_specs=(pl.BlockSpec(memory_space=pltpu.VMEM), pl.BlockSpec(memory_space=pltpu.VMEM)),
        scratch_shapes=[
            vmem(LAYERS, ROWS, C),
            vmem(LAYERS, ROWS, C),
            vmem(LAYERS, ROWS, C),
            vmem(ROWS, C),
            vmem(LAYERS, ROWS, C),
            vmem(LAYERS, 2, ROWS, C),
            vmem(LAYERS, TAPS, C, C),
            vmem(LAYERS, 4, TAPS, SIDE, SIDE, STRIP, 128),
            vmem(LAYERS, 2, TAPS, SIDE, SIDE, STRIP, 128),
            vmem(LAYERS, 2, 3, TAPS, SIDE, STRIP, 128),
            vmem(LAYERS, 2, TAPS, SIDE, STRIP, 128),
            vmem(LAYERS, 2, 3, TAPS, STRIP, 128),
            vmem(LAYERS, 2, TAPS, SIDE, 8, 128),
            vmem(LAYERS, 3, 2, TAPS, 8, 128),
            vmem(LAYERS, 2, TAPS, 8, 128),
            vmem(LAYERS, 2, TAPS, 8, 128),
            dma(CHUNKS, 6), dma(2), dma(LAYERS),
            dma(LAYERS, 2, CHUNKS), dma(LAYERS, 2, CHUNKS),
            dma(LAYERS, 3), dma(LAYERS, 3),
            dma(LAYERS, 3, 2, 3), dma(LAYERS, 3, 2, 3),
            dma(LAYERS, 2, 3), dma(LAYERS, 2, 3),
            dma(LAYERS, 3), dma(LAYERS, 3),
            dma(LAYERS), dma(LAYERS),
        ],
        name="distill",
        compiler_params=pltpu.CompilerParams(collective_id=0, has_side_effects=True, vmem_limit_bytes=61 * 1024 * 1024),
    )(features, preacts, teacher, cotangent, kernels)


def solution(mesh):
    in_specs = (P("seq", None), P(None, "seq", None), P(None, "seq", None), P("seq", None), P())
    out_specs = (P("seq", None), P(None, None, "seq", None))
    return jax.shard_map(shards, mesh=mesh, in_specs=in_specs, out_specs=out_specs, check_vma=False)
```

```python
import math

import jax
import jax.numpy as jnp
from jax import lax
from jax.experimental import pallas as pl
from jax.experimental.pallas import tpu as pltpu
from jax.sharding import PartitionSpec as P

LAYERS = 3
TAPS = 3
SIDE = 4
ROWS = 512
C = 512
CHUNKS = 4
CHUNK = ROWS // CHUNKS
STRIP = 32
SCALE = 1.0 / math.sqrt(65536)
MIMIC = 0.5
MESH = pl.DeviceIdType.MESH
F32 = jnp.float32
LIMIT = 61 * 1024 * 1024
PARTS = 4


def cdf_of(u):
    return 0.5 * (1.0 + lax.erf(u * (1.0 / math.sqrt(2.0))))


def density_of(u):
    return jnp.exp(-0.5 * u * u) * (1.0 / math.sqrt(2.0 * math.pi))


def dot(left, right, over):
    return lax.dot_general(
        left, right, (((over,), (over,)), ((), ())), precision=lax.Precision.HIGH, preferred_element_type=F32
    )


def kernel(
    feat, pre, tea, cot, ker, out, kgrad,
    xs, pb, tb, g, gu, rb, w, kg, pbuf, r1, t1, r2, t2, r3, v, r4,
    go_sem, ld, ldt, ldw, ss, rs, ps, pr, q1, q2, q3, s4, q4,
):
    me = lax.axis_index("seq")
    core = me % 2
    z = (me // 2) % SIDE
    x = (me // 8) % SIDE
    y = me // 32
    last = 127

    def device(yy, xx, zz):
        return ((yy * SIDE + xx) * SIDE + zz) * 2 + core

    mate = me + 1 - 2 * core
    across = device(y, x, (z + 2) % SIDE)
    low = z < 2
    forward = jnp.where(low, me + 8, me - 8)
    source = jnp.where(low, me - 8, me + 8)
    xp = [device(y, (x + j) % SIDE, z) for j in range(1, SIDE)]
    yp = [device((y + j) % SIDE, x, z) for j in range(1, SIDE)]
    zp = [device(y, x, (z + j) % SIDE) for j in range(1, SIDE)]

    barrier = pltpu.get_barrier_semaphore()
    always = [mate, *xp, *yp, *zp]
    for other in always:
        pl.semaphore_signal(barrier, inc=1, device_id=(other,), device_id_type=MESH)
    greeted = len(always)
    for by, ring in ((1, 2), (-1, 2), (2, 8), (-2, 8), (8, 32), (-8, 32)):
        there = jnp.logical_and(me % ring + by < 0, me + by >= 0)
        if by > 0:
            there = jnp.logical_and(me % ring + by >= ring, me + by <= last)

        @pl.when(there)
        def _():
            pl.semaphore_signal(barrier, inc=1, device_id=(me + by,), device_id_type=MESH)

        greeted = greeted + jnp.where(there, 1, 0)

    def rows(c):
        return pl.ds(c * CHUNK, CHUNK)

    loads = []
    for c in range(CHUNKS):
        r = rows(c)
        pairs = [(feat.at[r], xs.at[0, r]), (cot.at[r], g.at[r]), (tea.at[2, r], tb.at[2, r])]
        pairs += [(pre.at[i, r], pb.at[i, r]) for i in range(LAYERS)]
        loads.append([pltpu.make_async_copy(a, b, ld.at[c, n]) for n, (a, b) in enumerate(pairs)])
    for group in loads:
        for copy in group:
            copy.start()
    wload = [pltpu.make_async_copy(ker.at[i], w.at[i], ldw.at[i]) for i in range(LAYERS)]
    tload = [pltpu.make_async_copy(tea.at[i], tb.at[i], ldt.at[i]) for i in range(2)]
    wload[2].start()
    tload[1].start()
    wload[1].start()
    tload[0].start()
    wload[0].start()

    def missing(condition, ref):
        @pl.when(condition)
        def _():
            ref[...] = jnp.zeros((ROWS, C), F32)

    missing(jnp.logical_or(jnp.logical_and(low, me - 8 < 0), jnp.logical_and(z >= 2, me + 8 > last)), rb.at[2, 1])
    missing(me + 2 > last, rb.at[1, 0])
    missing(me - 2 < 0, rb.at[1, 1])
    missing(me + 1 > last, rb.at[0, 0])
    missing(me - 1 < 0, rb.at[0, 1])

    def shift(layer, way, c, src, target):
        return pltpu.make_async_remote_copy(
            src_ref=src.at[rows(c)],
            dst_ref=rb.at[layer, way, rows(c)],
            send_sem=ss.at[layer, way, c],
            recv_sem=rs.at[layer, way, c],
            device_id=(target,),
            device_id_type=MESH,
        )

    def strips(c, body):
        def step(n, carry):
            body(pl.ds(pl.multiple_of(c * CHUNK + n * STRIP, STRIP), STRIP))
            return carry

        lax.fori_loop(0, CHUNK // STRIP, step, 0)

    def first(r):
        state = xs[0, r]
        for i in range(2):
            p = pb[i, r]
            cdf = cdf_of(p)
            state = state + p * cdf
            xs[i + 1, r] = state
            pb[i, r] = cdf + p * density_of(p)
        p = pb[2, r]
        cdf = cdf_of(p)
        state = state + p * cdf
        grad = g[r] + MIMIC * (state - tb[2, r])
        g[r] = grad
        gu[2, r] = grad * (cdf + p * density_of(p))

    for c in range(CHUNKS):
        for copy in loads[c]:
            copy.wait()
        strips(c, first)
        if c == 0:
            pl.semaphore_wait(barrier, greeted)
        shift(2, 0, c, gu.at[2], across).start()

    def place(layer, q, k, value, add=False):
        value = value.reshape(SIDE, SIDE, SIDE, 8, 128)
        kg[layer, q, k] = kg[layer, q, k] + value if add else value

    def term(layer, k, ref, rows_of=slice(None), add=False):
        full = dot(xs[layer, rows_of], ref[rows_of], 0)
        for q in range(4):
            place(layer, q, k, full[:, q * 128 : (q + 1) * 128], add)

    def lanes(q):
        return pl.ds(q * 128, 128)

    def term_of_columns(k, ref, ab):
        both = dot(xs[0], jnp.concatenate([ref[:, lanes(ab)], ref[:, lanes(2 + ab)]], axis=1), 0)
        place(0, ab, k, both[:, :128])
        place(0, 2 + ab, k, both[:, 128:])

    def remote(src, dst, send, recv, target):
        return pltpu.make_async_remote_copy(
            src_ref=src, dst_ref=dst, send_sem=send, recv_sem=recv, device_id=(target,), device_id_type=MESH
        )

    where = {"x": x, "y": y, "z": z}
    peers = {"x": xp, "y": yp, "z": zp}

    def pair(layer, k, ab):
        return remote(kg.at[layer, 2 * (1 - core) + ab, k], pbuf.at[layer, ab, k], ps.at[layer, k, ab], pr.at[layer, k, ab], mate)

    def pair_sum(layer, k, ab):
        pair(layer, k, ab).wait()
        kg[layer, 2 * core + ab, k] = kg[layer, 2 * core + ab, k] + pbuf[layer, ab, k]

    def cut(n, layer, k, ab, path, at):
        held = (kg.at[layer, 2 * core + ab, k], t1.at[layer, ab, k], t2.at[layer, ab, k])[n]
        left = [axis for axis in "yxz" if axis not in path[:n]]
        return held.at[tuple(at if axis == path[n] else slice(None) for axis in left)]

    def stage(n, layer, k, ab, path):
        axis = path[n]
        return [
            remote(
                cut(n, layer, k, ab, path, (where[axis] + j) % SIDE), (r1, r2, r3)[n].at[layer, ab, k, j - 1],
                ps.at[layer, k, ab], (q1, q2, q3)[n].at[layer, k, ab], peers[axis][j - 1])
            for j in range(1, SIDE)
        ]

    def stage_sum(n, layer, k, ab, path):
        got = (r1, r2, r3)[n]
        all3 = got.at[layer, ab, k]
        remote(all3, all3, ps.at[layer, k, ab], (q1, q2, q3)[n].at[layer, k, ab], mate).wait()
        own = cut(n, layer, k, ab, path, where[path[n]])[...]
        total = own + got[layer, ab, k, 0] + got[layer, ab, k, 1] + got[layer, ab, k, 2]
        if n < 2:
            (t1, t2)[n][layer, ab, k] = total
        else:
            v[layer, ab, k] = total * SCALE

    def stage4(layer, ab):
        return [remote(v.at[layer, ab], r4.at[layer, ab], s4.at[layer, ab], q4.at[layer, ab], mate)]

    def finish(layer, ab):
        for copy in stage4(layer, ab):
            copy.wait()
        for k in range(TAPS):
            mine, other = v[layer, ab, k], r4[layer, ab, k]
            for half in range(2):
                whole = jnp.where(core == half, mine, other)
                kgrad[layer, k, :4, lanes(2 * half + ab)] = jnp.where(core == 0, whole[:4], whole[4:])

    def go(copies):
        for copy in copies:
            copy.start()

    def send_pair(layer, k, halves=(0, 1)):
        go([pair(layer, k, ab) for ab in halves])

    def start1(layer, units):
        for unit in units:
            pair_sum(layer, *unit[:2])
            go(stage(0, layer, *unit))

    def start2(layer, units):
        for unit in units:
            stage_sum(0, layer, *unit)
            go(stage(1, layer, *unit))

    def start3(layer, units):
        for unit in units:
            stage_sum(1, layer, *unit)
            go(stage(2, layer, *unit))

    def start4(layer, units):
        for ab in range(2):
            mine = [unit for unit in units if unit[1] == ab]
            for unit in mine:
                stage_sum(2, layer, *unit)
            if mine:
                go(stage4(layer, ab))

    near = jnp.where(low, 0, 2)
    far = 2 - near
    wload[2].wait()
    g[...] = g[...] + dot(gu[2], w[2, 1], 1)
    term(2, 1, gu.at[2])
    send_pair(2, 1)
    tload[1].wait()

    forwards = jnp.logical_and(forward >= 0, forward <= last)
    fed = jnp.logical_and(source >= 0, source <= last)

    def swapped(c):
        shift(2, 0, c, gu.at[2], across).wait_recv()

        @pl.when(forwards)
        def _():
            shift(2, 1, c, rb.at[2, 0], forward).start()

        g[rows(c)] = g[rows(c)] + dot(rb[2, 0, rows(c)], w[2, near], 1)

    def send(layer, c):
        step = 2**layer

        @pl.when(me - step >= 0)
        def _():
            shift(layer, 0, c, gu.at[layer], me - step).start()

        @pl.when(me + step <= last)
        def _():
            shift(layer, 1, c, gu.at[layer], me + step).start()

    def arrive(layer, c):
        step = 2**layer

        @pl.when(me + step <= last)
        def _():
            shift(layer, 0, c, gu.at[layer], me).wait_recv()

        @pl.when(me - step >= 0)
        def _():
            shift(layer, 1, c, gu.at[layer], me).wait_recv()

    def sent(layer, c):
        step = 2**layer

        @pl.when(me - step >= 0)
        def _():
            shift(layer, 0, c, gu.at[layer], me - step).wait_send()

        @pl.when(me + step <= last)
        def _():
            shift(layer, 1, c, gu.at[layer], me + step).wait_send()

    def next_gu(layer, c):
        def body(r):
            grad = g[r] + MIMIC * (xs[layer + 1, r] - tb[layer, r])
            g[r] = grad
            gu[layer, r] = grad * pb[layer, r]

        strips(c, body)

    def forwarded(c):
        @pl.when(fed)
        def _():
            shift(2, 1, c, rb.at[2, 0], forward).wait_recv()

        g[rows(c)] = g[rows(c)] + dot(rb[2, 1, rows(c)], w[2, far], 1)
        next_gu(1, c)

    units2 = [(k, ab, ("xyz", "yxz")[ab]) for k in (1, near, far) for ab in range(2)]
    start1(2, units2[:2])
    for c in range(CHUNKS + 1):
        if c < CHUNKS:
            swapped(c)
        if c == CHUNKS:
            term(2, near, rb.at[2, 0])
            send_pair(2, near)
        if c >= 1:
            forwarded(c - 1)
            if c >= CHUNKS - 2:
                send(1, c - 2)
            if c == CHUNKS:
                send(1, c - 1)
    term(2, far, rb.at[2, 1])
    send_pair(2, far)
    start1(2, units2[2:4])
    for c in range(CHUNKS):
        shift(2, 0, c, gu.at[2], across).wait_send()

        @pl.when(forwards)
        def _():
            shift(2, 1, c, rb.at[2, 0], forward).wait_send()

    wload[1].wait()
    tload[0].wait()
    g[...] = g[...] + dot(gu[1], w[1, 1], 1)
    term(1, 1, gu.at[1])
    send_pair(1, 1)
    start1(2, units2[4:])
    half = (slice(0, ROWS // 2), slice(ROWS // 2, ROWS))
    for c in range(CHUNKS):
        arrive(1, c)
        g[rows(c)] = g[rows(c)] + dot(rb[1, 0, rows(c)], w[1, 0], 1) + dot(rb[1, 1, rows(c)], w[1, 2], 1)
        next_gu(0, c)
        if c == 1:
            term(1, 0, rb.at[1, 0], half[0])
            term(1, 2, rb.at[1, 1], half[0])

    def across_chip(way, q):
        return remote(
            gu.at[0, :, lanes(q)], rb.at[0, way, :, lanes(q)], ss.at[0, way, q], rs.at[0, way, q], me - 1 if way == 0 else me + 1
        )

    order = ((0, 2), (1, 3))

    def each_way(groups, method):
        for q in groups:
            for way in range(2):
                here = (me - 1 >= 0) if way == 0 else (me + 1 <= last)
                if method == "wait_recv":
                    here = (me + 1 <= last) if way == 0 else (me - 1 >= 0)

                @pl.when(here)
                def _():
                    getattr(across_chip(way, q), method)()

    for groups in order:
        each_way(groups, "start")
    term(1, 0, rb.at[1, 0], half[1], True)
    send_pair(1, 0)
    term(1, 2, rb.at[1, 1], half[1], True)
    send_pair(1, 2)
    for c in range(CHUNKS):
        sent(1, c)
    wload[0].wait()
    term(0, 1, gu.at[0])
    send_pair(0, 1)
    units1 = [(0, 0, "xyz"), (0, 1, "yxz"), (2, 0, "xyz"), (2, 1, "yxz"), (1, 0, "zxy"), (1, 1, "zyx")]
    units0 = [(1, 0, "zxy"), (1, 1, "zyx"), (0, 0, "xyz"), (2, 0, "yxz"), (0, 1, "zxy"), (2, 1, "yxz")]
    start1(1, units1)
    start1(0, units0[:2])
    g[...] = g[...] + dot(gu[0], w[0, 1], 1)
    for ab, groups in enumerate(order):
        if ab == 1:
            start2(2, units2)
        each_way(groups, "wait_recv")
        term_of_columns(0, rb.at[0, 0], ab)
        send_pair(0, 0, (ab,))
        term_of_columns(2, rb.at[0, 1], ab)
        send_pair(0, 2, (ab,))
        if ab == 1:
            g[...] = g[...] + dot(rb[0, 0], w[0, 0], 1)
        start1(0, units0[2 + 2 * ab : 4 + 2 * ab])
    start3(2, units2)
    g[...] = g[...] + dot(rb[0, 1], w[0, 2], 1)
    start2(1, units1)
    start4(2, units2)
    result = pltpu.make_async_copy(g, out, go_sem)
    result.start()
    start2(0, units0[:4])
    start3(1, units1)
    start2(0, units0[4:])
    start3(0, units0[:4])
    start4(1, units1)
    finish(2, 0)
    finish(2, 1)
    start3(0, units0[4:])
    for groups in order:
        each_way(groups, "wait_send")
    start4(0, units0)
    finish(1, 0)
    finish(1, 1)
    finish(0, 0)
    finish(0, 1)
    result.wait()


def hand_over(grad, blocks, grad_out, kernel_grad_out, held, held_blocks, taken, given):
    part = ROWS // PARTS
    takes, gives = [], []
    for n in range(PARTS):
        r = pl.ds(n * part, part)
        takes.append(pltpu.make_async_copy(grad.at[r], held.at[r], taken.at[n]))
        gives.append(pltpu.make_async_copy(held.at[r], grad_out.at[r], given.at[n]))
    takes.append(pltpu.make_async_copy(blocks, held_blocks, taken.at[PARTS]))
    for copy in takes:
        copy.start()
    for n in range(PARTS):
        takes[n].wait()
        gives[n].start()
    takes[PARTS].wait()
    kernel_grad_out[...] = held_blocks[:, :, :4]
    for copy in gives:
        copy.wait()


def shards(features, preacts, teacher, cotangent, kernels):
    vmem = lambda *shape: pltpu.VMEM(shape, F32)
    dma = lambda *shape: pltpu.SemaphoreType.DMA(shape)
    grad, blocks = pl.pallas_call(
        kernel,
        out_shape=(
            jax.ShapeDtypeStruct((ROWS, C), F32),
            jax.ShapeDtypeStruct((LAYERS, TAPS, 8, C), F32),
        ),
        in_specs=[pl.BlockSpec(memory_space=pl.ANY)] * 5,
        out_specs=(pl.BlockSpec(memory_space=pl.ANY), pl.BlockSpec(memory_space=pltpu.VMEM)),
        scratch_shapes=[
            vmem(LAYERS, ROWS, C),
            vmem(LAYERS, ROWS, C),
            vmem(LAYERS, ROWS, C),
            vmem(ROWS, C),
            vmem(LAYERS, ROWS, C),
            vmem(LAYERS, 2, ROWS, C),
            vmem(LAYERS, TAPS, C, C),
            vmem(LAYERS, 4, TAPS, SIDE, SIDE, SIDE, 8, 128),
            vmem(LAYERS, 2, TAPS, SIDE, SIDE, SIDE, 8, 128),
            vmem(LAYERS, 2, TAPS, 3, SIDE, SIDE, 8, 128),
            vmem(LAYERS, 2, TAPS, SIDE, SIDE, 8, 128),
            vmem(LAYERS, 2, TAPS, 3, SIDE, 8, 128),
            vmem(LAYERS, 2, TAPS, SIDE, 8, 128),
            vmem(LAYERS, 2, TAPS, 3, 8, 128),
            vmem(LAYERS, 2, TAPS, 8, 128),
            vmem(LAYERS, 2, TAPS, 8, 128),
            pltpu.SemaphoreType.DMA, dma(CHUNKS, 6), dma(2), dma(LAYERS),
            dma(LAYERS, 2, CHUNKS), dma(LAYERS, 2, CHUNKS),
            dma(LAYERS, 3, 2), dma(LAYERS, 3, 2),
            dma(LAYERS, 3, 2), dma(LAYERS, 3, 2), dma(LAYERS, 3, 2),
            dma(LAYERS, 2), dma(LAYERS, 2),
        ],
        name="distill",
        compiler_params=pltpu.CompilerParams(collective_id=0, has_side_effects=True, vmem_limit_bytes=LIMIT),
    )(features, preacts, teacher, cotangent, kernels)
    return pl.pallas_call(
        hand_over,
        out_shape=(
            jax.ShapeDtypeStruct((ROWS, C), F32),
            jax.ShapeDtypeStruct((LAYERS, TAPS, 4, C), F32),
        ),
        in_specs=[pl.BlockSpec(memory_space=pl.ANY)] * 2,
        out_specs=(pl.BlockSpec(memory_space=pl.ANY), pl.BlockSpec(memory_space=pltpu.VMEM)),
        scratch_shapes=[vmem(ROWS, C), vmem(LAYERS, TAPS, 8, C), dma(PARTS + 1), dma(PARTS)],
        name="hand_over",
        compiler_params=pltpu.CompilerParams(vmem_limit_bytes=LIMIT),
    )(grad, blocks)


def solution(mesh):
    in_specs = (P("seq", None), P(None, "seq", None), P(None, "seq", None), P("seq", None), P())
    out_specs = (P("seq", None), P(None, None, "seq", None))
    return jax.shard_map(shards, mesh=mesh, in_specs=in_specs, out_specs=out_specs, check_vma=False)
```

```python
import math

import jax
import jax.numpy as jnp
from jax import lax
from jax.experimental import pallas as pl
from jax.experimental.pallas import tpu as pltpu
from jax.sharding import PartitionSpec as P

LAYERS = 3
TAPS = 3
SIDE = 4
ROWS = 512
C = 512
CHUNKS = 4
CHUNK = ROWS // CHUNKS
STRIP = 32
EARLY = 2
SCALE = 1.0 / math.sqrt(65536)
MIMIC = 0.5
MESH = pl.DeviceIdType.MESH
F32 = jnp.float32
LIMIT = 61 * 1024 * 1024
PARTS = 4


def cdf_of(u):
    return 0.5 * (1.0 + lax.erf(u * (1.0 / math.sqrt(2.0))))


def density_of(u):
    return jnp.exp(-0.5 * u * u) * (1.0 / math.sqrt(2.0 * math.pi))


def dot(left, right, over):
    return lax.dot_general(
        left, right, (((over,), (over,)), ((), ())), precision=lax.Precision.HIGH, preferred_element_type=F32
    )


def kernel(
    feat, pre, tea, cot, ker, out, kgrad,
    xs, pb, tb, g, gu, rb, w, kg, pbuf, r1, t1, r2, t2, r3, v, r4,
    go_sem, ld, ldt, ldw, ss, rs, cs, cr, ps, pr, q1, q2, q3, s4, q4,
):
    me = lax.axis_index("seq")
    core = me % 2
    z = (me // 2) % SIDE
    x = (me // 8) % SIDE
    y = me // 32
    last = 127

    def device(yy, xx, zz):
        return ((yy * SIDE + xx) * SIDE + zz) * 2 + core

    mate = me + 1 - 2 * core
    across = device(y, x, (z + 2) % SIDE)
    low = z < 2
    forward = jnp.where(low, me + 8, me - 8)
    source = jnp.where(low, me - 8, me + 8)
    xp = [device(y, (x + j) % SIDE, z) for j in range(1, SIDE)]
    yp = [device((y + j) % SIDE, x, z) for j in range(1, SIDE)]
    zp = [device(y, x, (z + j) % SIDE) for j in range(1, SIDE)]

    barrier = pltpu.get_barrier_semaphore()
    always = [mate, *xp, *yp, *zp]
    for other in always:
        pl.semaphore_signal(barrier, inc=1, device_id=(other,), device_id_type=MESH)
    greeted = len(always)
    for by, ring in ((1, 2), (-1, 2), (2, 8), (-2, 8), (8, 32), (-8, 32)):
        there = jnp.logical_and(me % ring + by < 0, me + by >= 0)
        if by > 0:
            there = jnp.logical_and(me % ring + by >= ring, me + by <= last)

        @pl.when(there)
        def _():
            pl.semaphore_signal(barrier, inc=1, device_id=(me + by,), device_id_type=MESH)

        greeted = greeted + jnp.where(there, 1, 0)

    def rows(c):
        return pl.ds(c * CHUNK, CHUNK)

    loads = []
    for c in range(CHUNKS):
        r = rows(c)
        pairs = [(feat.at[r], xs.at[0, r]), (cot.at[r], g.at[r]), (tea.at[2, r], tb.at[2, r])]
        pairs += [(pre.at[i, r], pb.at[i, r]) for i in range(LAYERS)]
        loads.append([pltpu.make_async_copy(a, b, ld.at[c, n]) for n, (a, b) in enumerate(pairs)])
    for group in loads:
        for copy in group:
            copy.start()
    wload = [pltpu.make_async_copy(ker.at[i], w.at[i], ldw.at[i]) for i in range(LAYERS)]
    tload = [pltpu.make_async_copy(tea.at[i], tb.at[i], ldt.at[i]) for i in range(2)]
    wload[2].start()
    tload[1].start()
    wload[1].start()
    tload[0].start()
    wload[0].start()

    def missing(condition, ref):
        @pl.when(condition)
        def _():
            ref[...] = jnp.zeros((ROWS, C), F32)

    missing(jnp.logical_or(jnp.logical_and(low, me - 8 < 0), jnp.logical_and(z >= 2, me + 8 > last)), rb.at[2, 1])
    missing(me + 2 > last, rb.at[1, 0])
    missing(me - 2 < 0, rb.at[1, 1])
    missing(me + 1 > last, rb.at[0, 0])
    missing(me - 1 < 0, rb.at[0, 1])

    def shift(layer, way, c, src, target):
        return pltpu.make_async_remote_copy(
            src_ref=src.at[rows(c)],
            dst_ref=rb.at[layer, way, rows(c)],
            send_sem=ss.at[layer - 1, way, c],
            recv_sem=rs.at[layer - 1, way, c],
            device_id=(target,),
            device_id_type=MESH,
        )

    def strips(c, body):
        def step(n, carry):
            body(pl.ds(pl.multiple_of(c * CHUNK + n * STRIP, STRIP), STRIP))
            return carry

        lax.fori_loop(0, CHUNK // STRIP, step, 0)

    def first(r):
        state = xs[0, r]
        for i in range(2):
            p = pb[i, r]
            cdf = cdf_of(p)
            state = state + p * cdf
            xs[i + 1, r] = state
            pb[i, r] = cdf + p * density_of(p)
        p = pb[2, r]
        cdf = cdf_of(p)
        state = state + p * cdf
        grad = g[r] + MIMIC * (state - tb[2, r])
        g[r] = grad
        gu[2, r] = grad * (cdf + p * density_of(p))

    for c in range(CHUNKS):
        for copy in loads[c]:
            copy.wait()
        strips(c, first)
        if c == 0:
            pl.semaphore_wait(barrier, greeted)
        shift(2, 0, c, gu.at[2], across).start()

    def place(layer, q, k, value, add=False):
        value = value.reshape(SIDE, SIDE, SIDE, 8, 128)
        kg[layer, q, k] = kg[layer, q, k] + value if add else value

    def term(layer, k, ref, rows_of=slice(None), add=False):
        full = dot(xs[layer, rows_of], ref[rows_of], 0)
        for q in range(4):
            place(layer, q, k, full[:, q * 128 : (q + 1) * 128], add)

    def lanes(q):
        return pl.ds(q * 128, 128)

    def term_of_columns(k, ref, ab):
        both = dot(xs[0], jnp.concatenate([ref[:, lanes(ab)], ref[:, lanes(2 + ab)]], axis=1), 0)
        place(0, ab, k, both[:, :128])
        place(0, 2 + ab, k, both[:, 128:])

    def remote(src, dst, send, recv, target):
        return pltpu.make_async_remote_copy(
            src_ref=src, dst_ref=dst, send_sem=send, recv_sem=recv, device_id=(target,), device_id_type=MESH
        )

    where = {"x": x, "y": y, "z": z}
    peers = {"x": xp, "y": yp, "z": zp}

    def pair(layer, k, ab):
        return remote(kg.at[layer, 2 * (1 - core) + ab, k], pbuf.at[layer, ab, k], ps.at[layer, k, ab], pr.at[layer, k, ab], mate)

    def pair_sum(layer, k, ab):
        pair(layer, k, ab).wait()
        kg[layer, 2 * core + ab, k] = kg[layer, 2 * core + ab, k] + pbuf[layer, ab, k]

    def cut(n, layer, k, ab, path, at):
        held = (kg.at[layer, 2 * core + ab, k], t1.at[layer, ab, k], t2.at[layer, ab, k])[n]
        left = [axis for axis in "yxz" if axis not in path[:n]]
        return held.at[tuple(at if axis == path[n] else slice(None) for axis in left)]

    def stage(n, layer, k, ab, path):
        axis = path[n]
        return [
            remote(
                cut(n, layer, k, ab, path, (where[axis] + j) % SIDE), (r1, r2, r3)[n].at[layer, ab, k, j - 1],
                ps.at[layer, k, ab], (q1, q2, q3)[n].at[layer, k, ab], peers[axis][j - 1])
            for j in range(1, SIDE)
        ]

    def stage_sum(n, layer, k, ab, path):
        got = (r1, r2, r3)[n]
        all3 = got.at[layer, ab, k]
        remote(all3, all3, ps.at[layer, k, ab], (q1, q2, q3)[n].at[layer, k, ab], mate).wait()
        own = cut(n, layer, k, ab, path, where[path[n]])[...]
        total = own + got[layer, ab, k, 0] + got[layer, ab, k, 1] + got[layer, ab, k, 2]
        if n < 2:
            (t1, t2)[n][layer, ab, k] = total
        else:
            v[layer, ab, k] = total * SCALE

    def stage4(layer, ab):
        return [remote(v.at[layer, ab], r4.at[layer, ab], s4.at[layer, ab], q4.at[layer, ab], mate)]

    def finish(layer, ab):
        for copy in stage4(layer, ab):
            copy.wait()
        for k in range(TAPS):
            mine, other = v[layer, ab, k], r4[layer, ab, k]
            for half in range(2):
                whole = jnp.where(core == half, mine, other)
                kgrad[layer, k, :4, lanes(2 * half + ab)] = jnp.where(core == 0, whole[:4], whole[4:])

    def go(copies):
        for copy in copies:
            copy.start()

    def send_pair(layer, k, halves=(0, 1)):
        go([pair(layer, k, ab) for ab in halves])

    def start1(layer, units):
        for unit in units:
            pair_sum(layer, *unit[:2])
            go(stage(0, layer, *unit))

    def start2(layer, units):
        for unit in units:
            stage_sum(0, layer, *unit)
            go(stage(1, layer, *unit))

    def start3(layer, units):
        for unit in units:
            stage_sum(1, layer, *unit)
            go(stage(2, layer, *unit))

    def start4(layer, units):
        for ab in range(2):
            mine = [unit for unit in units if unit[1] == ab]
            for unit in mine:
                stage_sum(2, layer, *unit)
            if mine:
                go(stage4(layer, ab))

    near = jnp.where(low, 0, 2)
    far = 2 - near
    wload[2].wait()
    g[...] = g[...] + dot(gu[2], w[2, 1], 1)
    term(2, 1, gu.at[2])
    send_pair(2, 1)
    tload[1].wait()

    forwards = jnp.logical_and(forward >= 0, forward <= last)
    fed = jnp.logical_and(source >= 0, source <= last)

    def swapped(c):
        shift(2, 0, c, gu.at[2], across).wait_recv()

        @pl.when(forwards)
        def _():
            shift(2, 1, c, rb.at[2, 0], forward).start()

        g[rows(c)] = g[rows(c)] + dot(rb[2, 0, rows(c)], w[2, near], 1)

    def send(layer, c):
        step = 2**layer

        @pl.when(me - step >= 0)
        def _():
            shift(layer, 0, c, gu.at[layer], me - step).start()

        @pl.when(me + step <= last)
        def _():
            shift(layer, 1, c, gu.at[layer], me + step).start()

    def arrive(layer, c):
        step = 2**layer

        @pl.when(me + step <= last)
        def _():
            shift(layer, 0, c, gu.at[layer], me).wait_recv()

        @pl.when(me - step >= 0)
        def _():
            shift(layer, 1, c, gu.at[layer], me).wait_recv()

    def sent(layer, c):
        step = 2**layer

        @pl.when(me - step >= 0)
        def _():
            shift(layer, 0, c, gu.at[layer], me - step).wait_send()

        @pl.when(me + step <= last)
        def _():
            shift(layer, 1, c, gu.at[layer], me + step).wait_send()

    def next_gu(layer, c):
        def body(r):
            grad = g[r] + MIMIC * (xs[layer + 1, r] - tb[layer, r])
            g[r] = grad
            gu[layer, r] = grad * pb[layer, r]

        strips(c, body)

    def forwarded(c):
        @pl.when(fed)
        def _():
            shift(2, 1, c, rb.at[2, 0], forward).wait_recv()

        g[rows(c)] = g[rows(c)] + dot(rb[2, 1, rows(c)], w[2, far], 1)
        next_gu(1, c)

    units2 = [(1, 0, "xyz"), (1, 1, "yxz"), (near, 0, "yxz"), (near, 1, "yxz"), (far, 0, "xyz"), (far, 1, "yxz")]
    start1(2, units2[:2])
    for c in range(CHUNKS + 1):
        if c < CHUNKS:
            swapped(c)
        if c == CHUNKS:
            term(2, near, rb.at[2, 0])
            send_pair(2, near)
        if c >= 1:
            forwarded(c - 1)
            if c >= CHUNKS - 2:
                send(1, c - 2)
            if c == CHUNKS:
                send(1, c - 1)
    term(2, far, rb.at[2, 1])
    send_pair(2, far)
    start1(2, units2[2:4])
    for c in range(CHUNKS):
        shift(2, 0, c, gu.at[2], across).wait_send()

        @pl.when(forwards)
        def _():
            shift(2, 1, c, rb.at[2, 0], forward).wait_send()

    wload[1].wait()
    tload[0].wait()
    g[...] = g[...] + dot(gu[1], w[1, 1], 1)
    term(1, 1, gu.at[1])
    send_pair(1, 1)
    start1(2, units2[4:])
    def across_chip(way, q, n):
        r = pl.ds(n * (ROWS // 2), ROWS // 2)
        return remote(
            gu.at[0, r, lanes(q)], rb.at[0, way, r, lanes(q)], cs.at[way, q, n], cr.at[way, q, n], me - 1 if way == 0 else me + 1
        )

    order = ((0, 2), (1, 3))

    def each_way(groups, method, parts=(0, 1)):
        for q in groups:
            for way in range(2):
                here = (me - 1 >= 0) if way == 0 else (me + 1 <= last)
                if method == "wait_recv":
                    here = (me + 1 <= last) if way == 0 else (me - 1 >= 0)

                @pl.when(here)
                def _():
                    for n in parts:
                        getattr(across_chip(way, q, n), method)()

    half = (slice(0, ROWS // 2), slice(ROWS // 2, ROWS))
    for c in range(CHUNKS):
        arrive(1, c)
        g[rows(c)] = g[rows(c)] + dot(rb[1, 0, rows(c)], w[1, 0], 1) + dot(rb[1, 1, rows(c)], w[1, 2], 1)
        next_gu(0, c)
        if c == 1:
            term(1, 0, rb.at[1, 0], half[0])
            term(1, 2, rb.at[1, 1], half[0])
        if c == EARLY:
            each_way(order[0], "start", (0,))

    each_way(order[0], "start", (1,))
    each_way(order[1], "start")
    term(1, 0, rb.at[1, 0], half[1], True)
    send_pair(1, 0)
    term(1, 2, rb.at[1, 1], half[1], True)
    send_pair(1, 2)
    for c in range(CHUNKS):
        sent(1, c)
    wload[0].wait()
    term(0, 1, gu.at[0])
    send_pair(0, 1)
    units1 = [(0, 0, "yxz"), (0, 1, "zxy"), (2, 0, "yxz"), (2, 1, "zyx"), (1, 0, "yxz"), (1, 1, "zyx")]
    units0 = [(1, 0, "zxy"), (1, 1, "zyx"), (0, 0, "xyz"), (2, 0, "xyz"), (0, 1, "xyz"), (2, 1, "yxz")]
    start1(1, units1)
    start1(0, units0[:2])
    g[...] = g[...] + dot(gu[0], w[0, 1], 1)
    for ab, groups in enumerate(order):
        if ab == 1:
            start2(2, units2)
        each_way(groups, "wait_recv")
        term_of_columns(0, rb.at[0, 0], ab)
        send_pair(0, 0, (ab,))
        term_of_columns(2, rb.at[0, 1], ab)
        send_pair(0, 2, (ab,))
        if ab == 1:
            g[...] = g[...] + dot(rb[0, 0], w[0, 0], 1)
        start1(0, units0[2 + 2 * ab : 4 + 2 * ab])
    g[...] = g[...] + dot(rb[0, 1], w[0, 2], 1)
    result = pltpu.make_async_copy(g, out, go_sem)
    start2(1, units1)
    result.start()
    start2(0, units0[:4])
    start3(2, units2)
    start2(0, units0[4:])
    start3(1, units1)
    start3(0, units0[:4])
    start4(2, units2)
    start3(0, units0[4:])
    for groups in order:
        each_way(groups, "wait_send")
    start4(1, units1)
    finish(2, 0)
    finish(2, 1)
    start4(0, units0)
    for layer in (1, 0):
        finish(layer, 0)
        finish(layer, 1)
    result.wait()


def hand_over(grad, blocks, grad_out, kernel_grad_out, held, held_blocks, taken, given):
    part = ROWS // PARTS
    takes, gives = [], []
    for n in range(PARTS):
        r = pl.ds(n * part, part)
        takes.append(pltpu.make_async_copy(grad.at[r], held.at[r], taken.at[n]))
        gives.append(pltpu.make_async_copy(held.at[r], grad_out.at[r], given.at[n]))
    takes.append(pltpu.make_async_copy(blocks, held_blocks, taken.at[PARTS]))
    for copy in takes:
        copy.start()
    for n in range(PARTS):
        takes[n].wait()
        gives[n].start()
    takes[PARTS].wait()
    kernel_grad_out[...] = held_blocks[:, :, :4]
    for copy in gives:
        copy.wait()


def shards(features, preacts, teacher, cotangent, kernels):
    vmem = lambda *shape: pltpu.VMEM(shape, F32)
    dma = lambda *shape: pltpu.SemaphoreType.DMA(shape)
    grad, blocks = pl.pallas_call(
        kernel,
        out_shape=(
            jax.ShapeDtypeStruct((ROWS, C), F32),
            jax.ShapeDtypeStruct((LAYERS, TAPS, 8, C), F32),
        ),
        in_specs=[pl.BlockSpec(memory_space=pl.ANY)] * 5,
        out_specs=(pl.BlockSpec(memory_space=pl.ANY), pl.BlockSpec(memory_space=pltpu.VMEM)),
        scratch_shapes=[
            vmem(LAYERS, ROWS, C),
            vmem(LAYERS, ROWS, C),
            vmem(LAYERS, ROWS, C),
            vmem(ROWS, C),
            vmem(LAYERS, ROWS, C),
            vmem(LAYERS, 2, ROWS, C),
            vmem(LAYERS, TAPS, C, C),
            vmem(LAYERS, 4, TAPS, SIDE, SIDE, SIDE, 8, 128),
            vmem(LAYERS, 2, TAPS, SIDE, SIDE, SIDE, 8, 128),
            vmem(LAYERS, 2, TAPS, 3, SIDE, SIDE, 8, 128),
            vmem(LAYERS, 2, TAPS, SIDE, SIDE, 8, 128),
            vmem(LAYERS, 2, TAPS, 3, SIDE, 8, 128),
            vmem(LAYERS, 2, TAPS, SIDE, 8, 128),
            vmem(LAYERS, 2, TAPS, 3, 8, 128),
            vmem(LAYERS, 2, TAPS, 8, 128),
            vmem(LAYERS, 2, TAPS, 8, 128),
            pltpu.SemaphoreType.DMA, dma(CHUNKS, 6), dma(2), dma(LAYERS),
            dma(2, 2, CHUNKS), dma(2, 2, CHUNKS), dma(2, 4, 2), dma(2, 4, 2),
            dma(LAYERS, 3, 2), dma(LAYERS, 3, 2),
            dma(LAYERS, 3, 2), dma(LAYERS, 3, 2), dma(LAYERS, 3, 2),
            dma(LAYERS, 2), dma(LAYERS, 2),
        ],
        name="distill",
        compiler_params=pltpu.CompilerParams(collective_id=0, has_side_effects=True, vmem_limit_bytes=LIMIT),
    )(features, preacts, teacher, cotangent, kernels)
    return pl.pallas_call(
        hand_over,
        out_shape=(
            jax.ShapeDtypeStruct((ROWS, C), F32),
            jax.ShapeDtypeStruct((LAYERS, TAPS, 4, C), F32),
        ),
        in_specs=[pl.BlockSpec(memory_space=pl.ANY)] * 2,
        out_specs=(pl.BlockSpec(memory_space=pl.ANY), pl.BlockSpec(memory_space=pltpu.VMEM)),
        scratch_shapes=[vmem(ROWS, C), vmem(LAYERS, TAPS, 8, C), dma(PARTS + 1), dma(PARTS)],
        name="hand_over",
        compiler_params=pltpu.CompilerParams(vmem_limit_bytes=LIMIT),
    )(grad, blocks)


def solution(mesh):
    in_specs = (P("seq", None), P(None, "seq", None), P(None, "seq", None), P("seq", None), P())
    out_specs = (P("seq", None), P(None, None, "seq", None))
    return jax.shard_map(shards, mesh=mesh, in_specs=in_specs, out_specs=out_specs, check_vma=False)
```
